32 devices in a mesh: context: 8 (over z, x), channel: 4 (over y, core).
Axes of the slice: x: 2, y: 2, z: 4, core: 2. Of those that a mesh axis runs over, the one named last changes fastest.
Arguments:
- inputs: bfloat16 [2048, 2048], P('channel', 'context'), may hold values from -6 to 6
- out_grad: bfloat16 [2048, 2048], P('channel', 'context'), may hold values from -6 to 6
- low_pass: float32 [2, 2048], P(None, 'channel'), may hold values from 0.75 to 1.25
- high_pass: float32 [2, 2048], P(None, 'channel'), may hold values from -3 to 3
- level_weight: float32 [12, 2048], P(None, 'channel'), may hold values from -1.75 to 1.75
- mix: bfloat16 [2048, 2048], P(None, 'channel'), may hold values from -0.125 to 0.125
Outputs:
- grad_inputs: bfloat16 [2048, 2048], P('channel', 'context')
- grad_low: float32 [2, 2048], P(None, 'channel')
- grad_high: float32 [2, 2048], P(None, 'channel')
- grad_level: float32 [12, 2048], P(None, 'channel')
- grad_mix: float32 [2048, 2048], P('context', 'channel')
The draws below stay inside these ranges and needn't reach their ends.
All inputs are finite; a program needn't handle non-finite values.
Results may differ from the reference program's by a relative error of at most 0.012.
Values may be sent and summed in bfloat16 or wider, within the bound.
A program may use at most 64 MiB of HBM per device.

```python
import jax
import jax.numpy as jnp
from jax import lax

D = 2048
LEVELS = 11
TOKENS = 2048
N_CHANNEL = 4


def steps_of(stream_key, shape, split, smallest, top_value):
    def one(position, blocks):
        heights = jax.random.uniform(jax.random.fold_in(jax.random.fold_in(stream_key, 6), position), (blocks,), jnp.float32, smallest / len(split), top_value / len(split))
        return jnp.repeat(jnp.exp(heights), shape[position] // blocks).reshape((-1,) + (1,) * (len(shape) - position - 1))

    factor_of = one(*split[0])
    for cut in split[1:]:
        factor_of = factor_of * one(*cut)
    return factor_of


def bell_draw(key, dims, scale, bound, pieces=(), kind=jnp.bfloat16):
    level = steps_of(key, dims, pieces, -0.22, 0.18) if pieces else 1.0
    drawn = jax.random.normal(key, dims, jnp.float32) * scale * level
    return jnp.minimum(jnp.maximum(drawn, -bound), bound).astype(kind)


def setup_inputs(seed: int = 0) -> dict:
    key_of = jax.random.split(jax.random.key(seed), 7)
    return {
        "inputs": bell_draw(key_of[0], (D, TOKENS), 1.0, 6.0, ((0, 4), (1, 8))),
        "out_grad": bell_draw(key_of[1], (D, TOKENS), 1.0, 6.0, ((0, 4), (1, 8))),
        "low_pass": jnp.clip(1.0 + 0.05 * jax.random.normal(key_of[2], (2, D), jnp.float32), 0.75, 1.25),
        "high_pass": bell_draw(key_of[3], (2, D), 1.0, 3.0, ((1, 4),), jnp.float32),
        "level_weight": bell_draw(key_of[4], (LEVELS + 1, D), (LEVELS + 1) ** -0.5, 1.75, ((1, 4),), jnp.float32),
        "mix": bell_draw(key_of[5], (D, D), D ** -0.5, 0.125, ((1, 4),)),
    }


HALF_ROOT = 0.5 ** 0.5

def later(values, distance):
    pad_zeros = jnp.zeros((values.shape[0], distance), values.dtype)
    return jnp.concatenate([pad_zeros, values[:, :values.shape[1] - distance]], 1)

def earlier(values, distance):
    pad_zeros = jnp.zeros((values.shape[0], distance), values.dtype)
    return jnp.concatenate([values[:, distance:], pad_zeros], 1)

def forward(present, low_taps, high_taps, weights):
    mixed_sum = jnp.zeros(present.shape, jnp.float32)
    pairs = []
    for level_index in range(LEVELS):
        lagged = later(present, 2 ** level_index)
        pairs.append((present, lagged))
        present_wide = present.astype(jnp.float32)
        lagged_wide = lagged.astype(jnp.float32)
        branch = HALF_ROOT * (high_taps[1 - 1] * present_wide + high_taps[1] * lagged_wide)
        present = (HALF_ROOT * (low_taps[0] * present_wide + low_taps[1] * lagged_wide)).astype(jnp.bfloat16)
        mixed_sum = mixed_sum + weights[level_index + 1] * branch
    mixed_sum = mixed_sum + weights[0] * present.astype(jnp.float32)
    return (mixed_sum, present, pairs)

def backward(args):
    present, grad_z, low_block, high_block, weight_block = args
    low_taps = low_block[:, :, None]
    high_taps = high_block[:, :, None]
    weights = weight_block[:, :, None]
    mixed_sum, last_level, pairs = forward(present, low_taps, high_taps, weights)
    grad_mixed = jax.vjp(jax.nn.gelu, mixed_sum)[1](grad_z)[0]
    low_acc = jnp.zeros((2, present.shape[0]), jnp.float32)
    high_acc = jnp.zeros((2, present.shape[0]), jnp.float32)
    rows_out = [None] * (LEVELS + 1)
    rows_out[0] = lax.optimization_barrier(jnp.sum(grad_mixed * last_level.astype(jnp.float32), 1))
    grad_now = weights[0] * grad_mixed
    for level_index in reversed(range(LEVELS)):
        level_now, lagged = pairs[level_index]
        present_wide = level_now.astype(jnp.float32)
        lagged_wide = lagged.astype(jnp.float32)
        grad_branch = weights[level_index + 1] * grad_mixed
        branch = HALF_ROOT * (high_taps[0] * present_wide + high_taps[1] * lagged_wide)
        low_acc = low_acc + HALF_ROOT * jnp.stack([lax.optimization_barrier(jnp.sum(present_wide * grad_now, 1)), lax.optimization_barrier(jnp.sum(lagged_wide * grad_now, 1))])
        high_acc = high_acc + HALF_ROOT * jnp.stack([lax.optimization_barrier(jnp.sum(present_wide * grad_branch, 1)), lax.optimization_barrier(jnp.sum(lagged_wide * grad_branch, 1))])
        rows_out[level_index + 1] = lax.optimization_barrier(jnp.sum(grad_mixed * branch, 1))
        direct_part = HALF_ROOT * (low_taps[0] * grad_now + high_taps[0] * grad_branch)
        lagged_part = HALF_ROOT * (low_taps[1] * grad_now + high_taps[1] * grad_branch)
        grad_now = direct_part + earlier(lagged_part, 2 ** level_index)
    return (grad_now.astype(jnp.bfloat16), low_acc, high_acc, jnp.stack(rows_out))

def reference(inputs, out_grad, low_pass, high_pass, level_weight, mix):
    block = D // (4 * N_CHANNEL)
    count = D // block

    def blocks_of(table):
        return table.reshape(table.shape[0], count, block).transpose(1, 0, 2)

    def unblock(table):
        return table.transpose(1, 0, 2).reshape(table.shape[1], D)
    inputs_blocks = inputs.reshape(count, block, TOKENS)
    low_blocks = blocks_of(low_pass)
    high_blocks = blocks_of(high_pass)
    weight_blocks = blocks_of(level_weight)

    def forward_z(args):
        present, low_block, high_block, weight_block = args
        mixed_sum = forward(present, low_block[:, :, None], high_block[:, :, None], weight_block[:, :, None])[0]
        return jax.nn.gelu(mixed_sum).astype(jnp.bfloat16)
    z_all = lax.map(forward_z, (inputs_blocks, low_blocks, high_blocks, weight_blocks)).reshape(D, TOKENS)
    scale = float(TOKENS) ** (-0.5)
    grad_mix = lax.dot_general(z_all, out_grad, (((1,), (1,)), ((), ())), preferred_element_type=jnp.float32) * scale
    grad_z = jnp.dot(mix, out_grad, preferred_element_type=jnp.float32)
    grad_x, low_grad, high_grad, level_grad = lax.map(backward, (inputs_blocks, grad_z.reshape(count, block, TOKENS), low_blocks, high_blocks, weight_blocks))
    return (grad_x.reshape(D, TOKENS), unblock(low_grad) * scale, unblock(high_grad) * scale, unblock(level_grad) * scale, grad_mix)
```

```python
import functools

import jax
import jax.numpy as jnp
from jax import lax
from jax.experimental import pallas as pl
from jax.experimental.pallas import tpu as pltpu
from jax.sharding import PartitionSpec as P

HALF_ROOT = 0.5**0.5
GELU_C = (2.0 / 3.141592653589793) ** 0.5
CHUNK = 8


def kernel(
    n, m, levels,
    x_ref, og_ref, prm_ref, mix_ref,
    gi_ref, small_ref, gmix_ref,
    xin, pbuf, mixr, og_all, gzs, gzr, gz, lv, lg, gp, zsend, zall, gibuf, accm, sbuf,
    mix_sem, xs_send, xs_recv, p_send, p_recv,
    up_send, dn_send, xb_send, xa_send, og_recv,
    gz_send, gz_recv, z_send, z_recv, gi_send, gi_recv, sm_send, sm_recv,
):
    i = lax.axis_index("context")
    j = lax.axis_index("channel")
    channels, length = x_ref.shape
    width = channels // n
    rows = width * m
    tokens = n * length
    lines = n // 2
    zi, xi = i // 2, i % 2
    mine = i * rows + j * width
    home = mine // channels
    slot = (mine % channels) // width
    here = home == j
    scale = float(tokens) ** (-0.5)

    def owner(b):
        g = j * channels + b * width
        return g // rows, (g % rows) // width

    def dev(a, b):
        return {"context": a, "channel": b}

    def remote(src, dst, ssem, rsem, a, b):
        return pltpu.make_async_remote_copy(
            src_ref=src, dst_ref=dst, send_sem=ssem, recv_sem=rsem,
            device_id=dev(a, b), device_id_type=pl.DeviceIdType.MESH,
        )

    mix_copy = pltpu.make_async_copy(
        mix_ref.at[pl.ds(pl.multiple_of(i * rows, 16), rows), :], mixr, mix_sem
    )
    mix_copy.start()

    barrier = pltpu.get_barrier_semaphore()

    def hello(a, b):
        pl.semaphore_signal(
            barrier, inc=1, device_id=dev(a, b), device_id_type=pl.DeviceIdType.MESH
        )

    for b in range(n):
        oi, oj = owner(b)
        pl.when(jnp.logical_or(oi != i, oj != j))(functools.partial(hello, oi, oj))
        pl.when(jnp.logical_or(b != i, home != j))(functools.partial(hello, b, home))
    for off in range(1, m):
        hello(i, (j + off) % m)
    hello(zi * 2 + 1 - xi, j)
    pl.when(zi > 0)(functools.partial(hello, i - 2, j))
    pl.when(zi < lines - 1)(functools.partial(hello, i + 2, j))
    expected = (
        2 * n + m
        - 2 * here.astype(jnp.int32)
        + (zi > 0).astype(jnp.int32)
        + (zi < lines - 1).astype(jnp.int32)
    )
    pl.semaphore_wait(barrier, expected)

    def prm_copy(b, oi, oj):
        return remote(
            prm_ref.at[pl.ds(b * width, width), :], pbuf, p_send.at[b], p_recv, oi, oj
        )

    def x_copy(b, oi, oj):
        return remote(
            x_ref.at[pl.ds(b * width, width), :], xin.at[i], xs_send.at[b], xs_recv.at[i], oi, oj
        )

    for b in range(n):
        oi, oj = owner(b)
        away = jnp.logical_or(oi != i, oj != j)

        @pl.when(away)
        def _():
            @pl.when(oi == i)
            def _():
                prm_copy(b, oi, oj).start()

            x_copy(b, oi, oj).start()

        @pl.when(jnp.logical_not(away))
        def _():
            pbuf[...] = prm_ref[pl.ds(b * width, width), :]
            xin[i] = x_ref[pl.ds(b * width, width), :]

    def block_copy(src, q, ssem, target):
        return remote(src, og_all.at[q], ssem, og_recv.at[q], target, j)

    across = zi * 2 + 1 - xi

    def up(src, q, s):
        return block_copy(src, q, up_send.at[s], i + 2)

    def down(src, q, s):
        return block_copy(src, q, dn_send.at[s], i - 2)

    has_up = zi < lines - 1
    has_down = zi > 0

    @pl.when(has_up)
    def _():
        up(og_ref, i, 0).start()

    @pl.when(has_down)
    def _():
        down(og_ref, i, 0).start()

    block_copy(og_ref, i, xb_send.at[0], across).start()
    og_all[i] = og_ref[...]
    mix_copy.wait()

    def gz_copy(d, q):
        return remote(gzs.at[d, q], gzr.at[j, q], gz_send.at[d, q], gz_recv.at[j, q], i, d)

    def partial_gz(q):
        full = jnp.dot(mixr[...], og_all[q], preferred_element_type=jnp.float32)
        for d in range(m):
            piece = full[d * width : (d + 1) * width]

            @pl.when(d == j)
            def _():
                gz[:, pl.ds(pl.multiple_of(q * length, 128), length)] = piece

            @pl.when(d != j)
            def _():
                gzs[d, q] = piece.astype(jnp.bfloat16)
                gz_copy(d, q).start()

    partial_gz(i)

    for a in range(n):
        @pl.when(jnp.logical_or(a != i, home != j))
        def _():
            pltpu.make_async_remote_copy(
                src_ref=xin.at[a], dst_ref=xin.at[a], send_sem=xs_send.at[0], recv_sem=xs_recv.at[a],
                device_id=dev(a, home), device_id_type=pl.DeviceIdType.MESH,
            ).wait_recv()

        lv[0, :, a * length : (a + 1) * length] = xin[a].astype(jnp.float32)

    @pl.when(jnp.logical_not(here))
    def _():
        remote(pbuf, pbuf, p_send.at[0], p_recv, i, home).wait_recv()

    lane = lax.broadcasted_iota(jnp.int32, (CHUNK, tokens), 1)

    def later(value, d):
        if d % 128 == 0:
            return jnp.concatenate(
                [jnp.zeros((CHUNK, d), value.dtype), value[:, : tokens - d]], 1
            )
        return jnp.where(lane < d, 0.0, pltpu.roll(value, d, 1))

    def earlier(value, d):
        if d % 128 == 0:
            return jnp.concatenate([value[:, d:], jnp.zeros((CHUNK, d), value.dtype)], 1)
        return jnp.where(lane >= tokens - d, 0.0, pltpu.roll(value, tokens - d, 1))

    def forward_chunk(c, carry):
        at = pl.ds(pl.multiple_of(c * CHUNK, CHUNK), CHUNK)
        prm = pbuf[at, :]
        l0, l1 = HALF_ROOT * prm[:, 0:1], HALF_ROOT * prm[:, 1:2]
        h0, h1 = HALF_ROOT * prm[:, 2:3], HALF_ROOT * prm[:, 3:4]
        now = lv[0, at, :]
        mixed = jnp.zeros((CHUNK, tokens), jnp.float32)
        for k in range(levels):
            w = prm[:, 5 + k : 6 + k]
            if 2**k >= tokens:
                lagged = jnp.zeros_like(now)
            else:
                lagged = later(now, 2**k)
            lg[k, at, :] = lagged
            mixed = mixed + ((w * h0) * now + (w * h1) * lagged)
            now = (l0 * now + l1 * lagged).astype(jnp.bfloat16).astype(jnp.float32)
            lv[k + 1, at, :] = now
        mixed = mixed + prm[:, 4:5] * now
        square = mixed * mixed
        t = jnp.tanh(GELU_C * (mixed * (1.0 + 0.044715 * square)))
        half = 0.5 * (1.0 + t)
        gp[at, :] = half + 0.5 * mixed * (1.0 - t * t) * (GELU_C * (1.0 + 0.134145 * square))
        lv[levels + 1, at, :] = mixed * half
        return carry

    lax.fori_loop(0, width // CHUNK, forward_chunk, 0)
    zsend[...] = lv[levels + 1].astype(jnp.bfloat16)
    zall[j] = zsend[...]

    def z_copy(off):
        return remote(
            zsend, zall.at[j], z_send.at[off], z_recv.at[j], i, (j + off) % m
        )

    def og_wait(q):
        block_copy(og_all.at[q], q, xb_send.at[0], across).wait_recv()

    def step(s, carry):
        below, above = zi - s, zi + s

        @pl.when(below >= 0)
        def _():
            q = below * 2 + xi
            og_wait(q)

            @pl.when(has_up)
            def _():
                up(og_all.at[q], q, s).start()

            block_copy(og_all.at[q], q, xb_send.at[s], across).start()

        @pl.when(above < lines)
        def _():
            q = above * 2 + xi
            og_wait(q)

            @pl.when(has_down)
            def _():
                down(og_all.at[q], q, s).start()

            block_copy(og_all.at[q], q, xa_send.at[s], across).start()

        @pl.when(below >= 0)
        def _():
            partial_gz(below * 2 + xi)

        @pl.when(above < lines)
        def _():
            partial_gz(above * 2 + xi)

        back, forth = zi - s + 1, zi + s - 1

        @pl.when(back >= 0)
        def _():
            q = back * 2 + 1 - xi
            og_wait(q)
            partial_gz(q)

        @pl.when(jnp.logical_and(forth < lines, s > 1))
        def _():
            q = forth * 2 + 1 - xi
            og_wait(q)
            partial_gz(q)

        return carry

    lax.fori_loop(1, lines, step, 0)
    for last in (zi - lines + 1, zi + lines - 1):
        @pl.when(jnp.logical_and(last >= 0, last < lines))
        def _():
            q = last * 2 + 1 - xi
            og_wait(q)
            partial_gz(q)

    for off in range(1, m):
        z_copy(off).start()

    def collect(q, carry):
        at = pl.ds(pl.multiple_of(q * length, 128), length)
        total = gz[:, at]
        for d in range(m):
            @pl.when(d != j)
            def _():
                remote(
                    gzs.at[d, q], gzr.at[d, q], gz_send.at[d, q], gz_recv.at[d, q], i, d
                ).wait()
        for off in range(1, m):
            total = total + gzr[(j + off) % m, q].astype(jnp.float32)
        gz[:, at] = total
        return carry

    lax.fori_loop(0, n, collect, 0)

    lanes = lax.broadcasted_iota(jnp.int32, (CHUNK, accm.shape[1]), 1)

    def backward_chunk(c, carry):
        at = pl.ds(pl.multiple_of(c * CHUNK, CHUNK), CHUNK)
        prm = pbuf[at, :]
        l0, l1 = HALF_ROOT * prm[:, 0:1], HALF_ROOT * prm[:, 1:2]
        h0, h1 = HALF_ROOT * prm[:, 2:3], HALF_ROOT * prm[:, 3:4]
        gm = gz[at, :] * gp[at, :]

        def total(value):
            return jnp.sum(value, axis=1, keepdims=True)

        out = jnp.where(lanes == 4, total(gm * lv[levels, at, :]), 0.0)
        grad = prm[:, 4:5] * gm
        zero = jnp.zeros((CHUNK, 1), jnp.float32)
        low0, low1, high0, high1 = zero, zero, zero, zero
        for k in reversed(range(levels)):
            w = prm[:, 5 + k : 6 + k]
            now, lagged = lv[k, at, :], lg[k, at, :]
            a, b = total(now * gm), total(lagged * gm)
            low0, low1 = low0 + total(now * grad), low1 + total(lagged * grad)
            high0, high1 = high0 + w * a, high1 + w * b
            out = out + jnp.where(lanes == 5 + k, h0 * a + h1 * b, 0.0)
            direct = l0 * grad + (h0 * w) * gm
            if 2**k < tokens:
                back = l1 * grad + (h1 * w) * gm
                direct = direct + earlier(back, 2**k)
            grad = direct
        for position, value in enumerate((low0, low1, high0, high1)):
            out = out + jnp.where(lanes == position, HALF_ROOT * value, 0.0)
        accm[at, :] = out * scale
        gz[at, :] = grad
        return carry

    lax.fori_loop(0, width // CHUNK, backward_chunk, 0)

    place = pl.ds(pl.multiple_of(slot * width, 16), width)

    def gi_copy(a):
        return remote(
            gibuf.at[a], gi_ref.at[place, :], gi_send.at[a], gi_recv.at[slot], a, home
        )

    def sm_copy(a):
        return remote(sbuf, small_ref.at[slot], sm_send.at[a], sm_recv.at[slot], a, home)

    turned = accm[...].T
    sbuf[...] = turned[: sbuf.shape[0], :]
    for a in range(n):
        gibuf[a] = gz[:, a * length : (a + 1) * length].astype(jnp.bfloat16)
        away = jnp.logical_or(a != i, home != j)

        @pl.when(away)
        def _():
            gi_copy(a).start()
            sm_copy(a).start()

        @pl.when(jnp.logical_not(away))
        def _():
            gi_ref[place, :] = gibuf[a]
            small_ref[slot] = sbuf[...]

    for off in range(1, m):
        src = (j + off) % m
        remote(zsend, zall.at[src], z_send.at[off], z_recv.at[src], i, src).wait_recv()
    for d in range(m):
        total = jnp.zeros((width, channels), jnp.float32)
        for q in range(n):
            total = total + lax.dot_general(
                zall[d, :, q * length : (q + 1) * length], og_all[q],
                (((1,), (1,)), ((), ())), preferred_element_type=jnp.float32,
            )
        gmix_ref[d * width : (d + 1) * width, :] = total * scale

    for b in range(n):
        oi, oj = owner(b)

        @pl.when(jnp.logical_or(oi != i, oj != j))
        def _():
            @pl.when(oi == i)
            def _():
                prm_copy(b, oi, oj).wait_send()

            x_copy(b, oi, oj).wait_send()
            there = pl.ds(b * width, width)
            remote(gibuf.at[b], gi_ref.at[there, :], gi_send.at[b], gi_recv.at[b], oi, oj).wait_recv()
            remote(sbuf, small_ref.at[b], sm_send.at[b], sm_recv.at[b], oi, oj).wait_recv()

        @pl.when(jnp.logical_or(b != i, home != j))
        def _():
            gi_copy(b).wait_send()
            sm_copy(b).wait_send()

    for off in range(1, m):
        z_copy(off).wait_send()

    def sent(s, carry):
        @pl.when(jnp.logical_and(zi - s >= 0, has_up))
        def _():
            up(og_ref, i, s).wait_send()

        @pl.when(jnp.logical_and(zi + s < lines, has_down))
        def _():
            down(og_ref, i, s).wait_send()

        @pl.when(zi - s >= 0)
        def _():
            block_copy(og_ref, i, xb_send.at[s], across).wait_send()

        @pl.when(jnp.logical_and(zi + s < lines, s > 0))
        def _():
            block_copy(og_ref, i, xa_send.at[s], across).wait_send()

        return carry

    lax.fori_loop(0, lines, sent, 0)


def solution(mesh):
    n, m = mesh.shape["context"], mesh.shape["channel"]

    def shards(inputs, out_grad, low_pass, high_pass, level_weight, mix):
        channels, length = inputs.shape
        levels = level_weight.shape[0] - 1
        width = channels // n
        rows, tokens, lines = width * m, n * length, n // 2
        count = 4 + levels + 1
        tall = -(-count // 8) * 8
        wide = -(-count // 128) * 128
        prm = jnp.concatenate([low_pass, high_pass, level_weight], 0).T
        prm = jnp.pad(prm, ((0, 0), (0, wide - count)))
        vmem = pl.BlockSpec(memory_space=pltpu.VMEM)
        f32, bf16 = jnp.float32, jnp.bfloat16
        sem = pltpu.SemaphoreType.DMA
        padded = -(-width // 128) * 128
        gi, small, gmix = pl.pallas_call(
            functools.partial(kernel, n, m, levels),
            out_shape=(
                jax.ShapeDtypeStruct((channels, length), bf16),
                jax.ShapeDtypeStruct((n, tall, padded), f32),
                jax.ShapeDtypeStruct((rows, channels), f32),
            ),
            in_specs=[vmem, vmem, vmem, pl.BlockSpec(memory_space=pl.ANY)],
            out_specs=(vmem, vmem, vmem),
            scratch_shapes=[
                pltpu.VMEM((n, width, length), bf16),
                pltpu.VMEM((width, wide), f32),
                pltpu.VMEM((rows, channels), bf16),
                pltpu.VMEM((n, channels, length), bf16),
                pltpu.VMEM((m, n, width, length), bf16),
                pltpu.VMEM((m, n, width, length), bf16),
                pltpu.VMEM((width, tokens), f32),
                pltpu.VMEM((levels + 2, width, tokens), f32),
                pltpu.VMEM((levels, width, tokens), f32),
                pltpu.VMEM((width, tokens), f32),
                pltpu.VMEM((width, tokens), bf16),
                pltpu.VMEM((m, width, tokens), bf16),
                pltpu.VMEM((n, width, length), bf16),
                pltpu.VMEM((padded, wide), f32),
                pltpu.VMEM((tall, padded), f32),
                sem, sem((n,)), sem((n,)), sem((n,)), sem,
                sem((lines,)), sem((lines,)), sem((lines,)), sem((lines,)), sem((n,)),
                sem((m, n)), sem((m, n)), sem((m,)), sem((m,)),
                sem((n,)), sem((n,)), sem((n,)), sem((n,)),
            ],
            compiler_params=pltpu.CompilerParams(collective_id=0, has_side_effects=True),
        )(inputs, out_grad, prm, mix)
        table = small[:, :count, :width].transpose(1, 0, 2).reshape(count, channels)
        return gi, table[0:2], table[2:4], table[4:], gmix

    return jax.shard_map(
        shards,
        mesh=mesh,
        in_specs=(
            P("channel", "context"),
            P("channel", "context"),
            P(None, "channel"),
            P(None, "channel"),
            P(None, "channel"),
            P(None, "channel"),
        ),
        out_specs=(
            P("channel", "context"),
            P(None, "channel"),
            P(None, "channel"),
            P(None, "channel"),
            P("context", "channel"),
        ),
        check_vma=False,
    )
```

```python
import functools

import jax
import jax.numpy as jnp
from jax import lax
from jax.experimental import pallas as pl
from jax.experimental.pallas import tpu as pltpu
from jax.sharding import PartitionSpec as P

HALF_ROOT = 0.5**0.5
GELU_C = (2.0 / 3.141592653589793) ** 0.5
CHUNK = 8
SEND = 0
RELAY = 0
AHEAD = 2
RELAY_EARLY = True


def kernel(
    n, m, levels,
    x_ref, og_ref, prm_ref, mix_ref,
    gi_ref, table_ref, gmix_ref,
    small, stage, xr_send, st_recv, xin, pbuf, mixr, og_all, gzs, gzr, gz, lv, lg, gp, zsend, zall, gibuf, accm, sbuf,
    mix_sem, xs_send, xs_recv, p_send, p_recv,
    up_send, dn_send, xb_send, xa_send, og_recv,
    gz_send, gz_recv, z_send, z_recv, gi_send, gi_recv, sm_send, sm_recv,
):
    i = lax.axis_index("context")
    j = lax.axis_index("channel")
    channels, length = x_ref.shape
    width = channels // n
    rows = width * m
    tokens = n * length
    lines = n // 2
    zi, xi = i // 2, i % 2
    mine = i * rows + j * width
    home = mine // channels
    slot = (mine % channels) // width
    here = home == j
    scale = float(tokens) ** (-0.5)

    xor1, xor2 = j + 1 - 2 * (j % 2), (j + 2) % m
    side = j // 2
    near = home // 2 == side
    sender = jnp.where(near, home, (home + 2) % m)

    def owner_of(shard, b):
        g = shard * channels + b * width
        return g // rows, (g % rows) // width

    def owner(b):
        return owner_of(j, b)

    def dev(a, b):
        return {"context": a, "channel": b}

    def remote(src, dst, ssem, rsem, a, b):
        return pltpu.make_async_remote_copy(
            src_ref=src, dst_ref=dst, send_sem=ssem, recv_sem=rsem,
            device_id=dev(a, b), device_id_type=pl.DeviceIdType.MESH,
        )

    mix_copy = pltpu.make_async_copy(
        mix_ref.at[pl.ds(pl.multiple_of(i * rows, 16), rows), :], mixr, mix_sem
    )
    mix_copy.start()

    barrier = pltpu.get_barrier_semaphore()

    def hello(a, b):
        pl.semaphore_signal(
            barrier, inc=1, device_id=dev(a, b), device_id_type=pl.DeviceIdType.MESH
        )

    expected = m
    for off in range(1, m):
        hello(i, (j + off) % m)
    hello(zi * 2 + 1 - xi, j)
    greetings = [(zi > 0, i - 2, j), (zi < lines - 1, i + 2, j)]
    for b in range(n):
        oi, oj = owner(b)
        greetings.append((jnp.logical_or(oi != i, oj != j), oi, oj))
        greetings.append((jnp.logical_or(b != i, home != j), b, home))
        oi, oj = owner_of(xor2, b)
        away = jnp.logical_or(oi != i, oj != j)
        greetings.append((jnp.logical_and(oj // 2 == side, away), oi, oj))
        away = jnp.logical_or(b != i, sender != j)
        greetings.append((jnp.logical_and(jnp.logical_not(near), away), b, sender))
    for wanted, a, b in greetings:
        pl.when(wanted)(functools.partial(hello, a, b))
        expected = expected + jnp.where(wanted, 1, 0)
    pl.semaphore_wait(barrier, expected)

    def prm_copy(b, oi, oj):
        return remote(
            prm_ref.at[pl.ds(b * width, width), :], pbuf, p_send.at[b], p_recv, oi, oj
        )

    def x_copy(b, oi, oj):
        return remote(
            x_ref.at[pl.ds(b * width, width), :], xin.at[i], xs_send.at[b], xs_recv.at[i], oi, oj
        )

    def stage_copy(b):
        return remote(
            x_ref.at[pl.ds(b * width, width), :], stage.at[b], xs_send.at[b], st_recv.at[b], i, xor2
        )

    def relay_copy(b, oi, oj):
        return remote(stage.at[b], xin.at[i], xr_send.at[b], xs_recv.at[i], oi, oj)

    def relay_inputs():
        for b in range(n):
            oi, oj = owner_of(xor2, b)

            @pl.when(oj // 2 == side)
            def _():
                stage_copy(b).wait_recv()

                @pl.when(jnp.logical_or(oi != i, oj != j))
                def _():
                    relay_copy(b, oi, oj).start()

                @pl.when(jnp.logical_and(oi == i, oj == j))
                def _():
                    xin[i] = stage[b]

    def send_inputs():
        for b in range(n):
            oi, oj = owner(b)
            away = jnp.logical_or(oi != i, oj != j)

            @pl.when(away)
            def _():
                @pl.when(oi == i)
                def _():
                    prm_copy(b, oi, oj).start()

                @pl.when(oj // 2 == side)
                def _():
                    x_copy(b, oi, oj).start()

                @pl.when(oj // 2 != side)
                def _():
                    stage_copy(b).start()

            @pl.when(jnp.logical_not(away))
            def _():
                pbuf[...] = prm_ref[pl.ds(b * width, width), :]
                xin[i] = x_ref[pl.ds(b * width, width), :]

    def block_copy(src, q, ssem, target):
        return remote(src, og_all.at[q], ssem, og_recv.at[q], target, j)

    across = zi * 2 + 1 - xi

    def up(src, q, s):
        return block_copy(src, q, up_send.at[s], i + 2)

    def down(src, q, s):
        return block_copy(src, q, dn_send.at[s], i - 2)

    has_up = zi < lines - 1
    has_down = zi > 0

    @pl.when(has_up)
    def _():
        up(og_ref, i, 0).start()

    @pl.when(has_down)
    def _():
        down(og_ref, i, 0).start()

    block_copy(og_ref, i, xb_send.at[0], across).start()
    og_all[i] = og_ref[...]
    mix_copy.wait()

    def gz_copy(d, q):
        return remote(gzs.at[d, q], gzr.at[j, q], gz_send.at[d, q], gz_recv.at[j, q], i, d)

    def partial_gz(q):
        full = jnp.dot(mixr[...], og_all[q], preferred_element_type=jnp.float32)
        for d in range(m):
            piece = full[d * width : (d + 1) * width]

            @pl.when(d == j)
            def _():
                gz[:, pl.ds(pl.multiple_of(q * length, 128), length)] = piece

            @pl.when(d != j)
            def _():
                gzs[d, q] = piece.astype(jnp.bfloat16)
                gz_copy(d, q).start()

    lane = lax.broadcasted_iota(jnp.int32, (CHUNK, tokens), 1)

    def later(value, d):
        if d % 128 == 0:
            return jnp.concatenate(
                [jnp.zeros((CHUNK, d), value.dtype), value[:, : tokens - d]], 1
            )
        return jnp.where(lane < d, 0.0, pltpu.roll(value, d, 1))

    def earlier(value, d):
        if d % 128 == 0:
            return jnp.concatenate([value[:, d:], jnp.zeros((CHUNK, d), value.dtype)], 1)
        return jnp.where(lane >= tokens - d, 0.0, pltpu.roll(value, tokens - d, 1))

    def forward_chunk(c, carry):
        at = pl.ds(pl.multiple_of(c * CHUNK, CHUNK), CHUNK)
        prm = pbuf[at, :]
        l0, l1 = HALF_ROOT * prm[:, 0:1], HALF_ROOT * prm[:, 1:2]
        h0, h1 = HALF_ROOT * prm[:, 2:3], HALF_ROOT * prm[:, 3:4]
        now = lv[0, at, :]
        mixed = jnp.zeros((CHUNK, tokens), jnp.float32)
        for k in range(levels):
            w = prm[:, 5 + k : 6 + k]
            if 2**k >= tokens:
                lagged = jnp.zeros_like(now)
            else:
                lagged = later(now, 2**k)
            lg[k, at, :] = lagged
            mixed = mixed + ((w * h0) * now + (w * h1) * lagged)
            now = (l0 * now + l1 * lagged).astype(jnp.bfloat16).astype(jnp.float32)
            lv[k + 1, at, :] = now
        mixed = mixed + prm[:, 4:5] * now
        square = mixed * mixed
        t = jnp.tanh(GELU_C * (mixed * (1.0 + 0.044715 * square)))
        half = 0.5 * (1.0 + t)
        gp[at, :] = half + 0.5 * mixed * (1.0 - t * t) * (GELU_C * (1.0 + 0.134145 * square))
        lv[levels + 1, at, :] = mixed * half
        return carry

    def z_copy(src, who, k, target):
        return remote(src, zall.at[who], z_send.at[k], z_recv.at[who], i, target)

    def z_start():
        z_copy(zsend, j, 0, xor1).start()
        z_copy(zsend, j, 1, xor2).start()

    def z_relay():
        z_copy(zsend, xor2, 1, xor2).wait_recv()
        z_copy(zall.at[xor2], xor2, 2, xor1).start()

    def z_arrive():
        z_copy(zsend, xor1, 0, xor1).wait_recv()
        z_copy(zsend, (xor1 + 2) % m, 2, xor1).wait_recv()

    def z_finish():
        z_copy(zsend, j, 0, xor1).wait_send()
        z_copy(zsend, j, 1, xor2).wait_send()
        z_copy(zsend, j, 2, xor1).wait_send()

    def forward():
        for a in range(n):
            @pl.when(jnp.logical_or(a != i, sender != j))
            def _():
                pltpu.make_async_remote_copy(
                    src_ref=xin.at[a], dst_ref=xin.at[a], send_sem=xs_send.at[0], recv_sem=xs_recv.at[a],
                    device_id=dev(a, sender), device_id_type=pl.DeviceIdType.MESH,
                ).wait_recv()

            lv[0, :, a * length : (a + 1) * length] = xin[a].astype(jnp.float32)

        @pl.when(jnp.logical_not(here))
        def _():
            remote(pbuf, pbuf, p_send.at[0], p_recv, i, home).wait_recv()

        lax.fori_loop(0, width // CHUNK, forward_chunk, 0)
        zsend[...] = lv[levels + 1].astype(jnp.bfloat16)
        zall[j] = zsend[...]
        z_start()

    def og_wait(q):
        block_copy(og_all.at[q], q, xb_send.at[0], across).wait_recv()

    def step(s, carry):
        below, above = zi - s, zi + s

        @pl.when(below >= 0)
        def _():
            q = below * 2 + xi
            og_wait(q)

            @pl.when(has_up)
            def _():
                up(og_all.at[q], q, s).start()

            block_copy(og_all.at[q], q, xb_send.at[s], across).start()

        @pl.when(above < lines)
        def _():
            q = above * 2 + xi
            og_wait(q)

            @pl.when(has_down)
            def _():
                down(og_all.at[q], q, s).start()

            block_copy(og_all.at[q], q, xa_send.at[s], across).start()

        @pl.when(below >= 0)
        def _():
            partial_gz(below * 2 + xi)

        @pl.when(above < lines)
        def _():
            partial_gz(above * 2 + xi)

        back, forth = zi - s + 1, zi + s - 1

        @pl.when(back >= 0)
        def _():
            q = back * 2 + 1 - xi
            og_wait(q)
            partial_gz(q)

        @pl.when(jnp.logical_and(forth < lines, s > 1))
        def _():
            q = forth * 2 + 1 - xi
            og_wait(q)
            partial_gz(q)

        return carry

    def steps(first, last):
        if last > first:
            lax.fori_loop(first, last, step, 0)

    if SEND == 0:
        send_inputs()
    partial_gz(i)
    if RELAY == 0:
        relay_inputs()
    if AHEAD == 0:
        forward()
    marks = sorted({1, min(SEND, lines - 1) + 1, min(AHEAD, lines - 1) + 1, min(RELAY, lines - 1) + 1, lines})
    for first, last in zip(marks[:-1], marks[1:]):
        steps(first, last)
        if last - 1 == min(SEND, lines - 1) and SEND > 0:
            send_inputs()
        if last - 1 == min(RELAY, lines - 1) and RELAY > 0:
            relay_inputs()
        if last - 1 == min(AHEAD, lines - 1) and AHEAD > 0:
            forward()
    for last in (zi - lines + 1, zi + lines - 1):
        @pl.when(jnp.logical_and(last >= 0, last < lines))
        def _():
            q = last * 2 + 1 - xi
            og_wait(q)
            partial_gz(q)

    if RELAY_EARLY:
        z_relay()
    def collect(q, carry):
        at = pl.ds(pl.multiple_of(q * length, 128), length)
        total = gz[:, at]
        for d in range(m):
            @pl.when(d != j)
            def _():
                remote(
                    gzs.at[d, q], gzr.at[d, q], gz_send.at[d, q], gz_recv.at[d, q], i, d
                ).wait()
        for off in range(1, m):
            total = total + gzr[(j + off) % m, q].astype(jnp.float32)
        gz[:, at] = total
        return carry

    lax.fori_loop(0, n, collect, 0)

    lanes = lax.broadcasted_iota(jnp.int32, (CHUNK, accm.shape[1]), 1)

    def backward_chunk(c, carry):
        at = pl.ds(pl.multiple_of(c * CHUNK, CHUNK), CHUNK)
        prm = pbuf[at, :]
        l0, l1 = HALF_ROOT * prm[:, 0:1], HALF_ROOT * prm[:, 1:2]
        h0, h1 = HALF_ROOT * prm[:, 2:3], HALF_ROOT * prm[:, 3:4]
        gm = gz[at, :] * gp[at, :]

        def fold(value):
            while value.shape[1] % 256 == 0:
                half = value.shape[1] // 2
                value = value[:, :half] + value[:, half:]
            parts = [value[:, p : p + 128] for p in range(0, value.shape[1], 128)]
            return sum(parts[1:], parts[0])

        def total(value):
            return jnp.sum(value, axis=1, keepdims=True)

        out = jnp.where(lanes == 4, total(fold(gm * lv[levels, at, :])), 0.0)
        grad = prm[:, 4:5] * gm
        zero = jnp.zeros((CHUNK, 128), jnp.float32)
        low0, low1, high0, high1 = zero, zero, zero, zero
        for k in reversed(range(levels)):
            w = prm[:, 5 + k : 6 + k]
            now, lagged = lv[k, at, :], lg[k, at, :]
            a, b = fold(now * gm), fold(lagged * gm)
            low0, low1 = low0 + fold(now * grad), low1 + fold(lagged * grad)
            high0, high1 = high0 + w * a, high1 + w * b
            out = out + jnp.where(lanes == 5 + k, total(h0 * a + h1 * b), 0.0)
            direct = l0 * grad + (h0 * w) * gm
            if 2**k < tokens:
                back = l1 * grad + (h1 * w) * gm
                direct = direct + earlier(back, 2**k)
            grad = direct
        for position, value in enumerate((low0, low1, high0, high1)):
            out = out + jnp.where(lanes == position, HALF_ROOT * total(value), 0.0)
        accm[at, :] = out * scale
        gz[at, :] = grad
        return carry

    lax.fori_loop(0, width // CHUNK, backward_chunk, 0)

    place = pl.ds(pl.multiple_of(slot * width, 16), width)

    def gi_copy(a):
        return remote(
            gibuf.at[a], gi_ref.at[place, :], gi_send.at[a], gi_recv.at[slot], a, home
        )

    def sm_copy(a):
        return remote(sbuf, small.at[slot], sm_send.at[a], sm_recv.at[slot], a, home)

    turned = accm[...].T
    sbuf[...] = turned[: sbuf.shape[0], :]
    for a in range(n):
        gibuf[a] = gz[:, a * length : (a + 1) * length].astype(jnp.bfloat16)
        away = jnp.logical_or(a != i, home != j)

        @pl.when(away)
        def _():
            gi_copy(a).start()
            sm_copy(a).start()

        @pl.when(jnp.logical_not(away))
        def _():
            gi_ref[place, :] = gibuf[a]
            small[slot] = sbuf[...]

    if not RELAY_EARLY:
        z_relay()
    z_arrive()
    for d in range(m):
        total = jnp.zeros((width, channels), jnp.float32)
        for q in range(n):
            total = total + lax.dot_general(
                zall[d, :, q * length : (q + 1) * length], og_all[q],
                (((1,), (1,)), ((), ())), preferred_element_type=jnp.float32,
            )
        gmix_ref[d * width : (d + 1) * width, :] = total * scale

    for b in range(n):
        oi, oj = owner(b)

        @pl.when(jnp.logical_or(oi != i, oj != j))
        def _():
            @pl.when(oi == i)
            def _():
                prm_copy(b, oi, oj).wait_send()

            x_copy(b, oi, oj).wait_send()
            there = pl.ds(b * width, width)
            remote(gibuf.at[b], gi_ref.at[there, :], gi_send.at[b], gi_recv.at[b], oi, oj).wait_recv()
            remote(sbuf, small.at[b], sm_send.at[b], sm_recv.at[b], oi, oj).wait_recv()

        ri, rj = owner_of(xor2, b)

        @pl.when(jnp.logical_and(rj // 2 == side, jnp.logical_or(ri != i, rj != j)))
        def _():
            relay_copy(b, ri, rj).wait_send()

        @pl.when(jnp.logical_or(b != i, home != j))
        def _():
            gi_copy(b).wait_send()
            sm_copy(b).wait_send()

    for b in range(n):
        part = pl.ds(b * width, width)
        table_ref[:, part] = small[b, :, :width]

    z_finish()

    def sent(s, carry):
        @pl.when(jnp.logical_and(zi - s >= 0, has_up))
        def _():
            up(og_ref, i, s).wait_send()

        @pl.when(jnp.logical_and(zi + s < lines, has_down))
        def _():
            down(og_ref, i, s).wait_send()

        @pl.when(zi - s >= 0)
        def _():
            block_copy(og_ref, i, xb_send.at[s], across).wait_send()

        @pl.when(jnp.logical_and(zi + s < lines, s > 0))
        def _():
            block_copy(og_ref, i, xa_send.at[s], across).wait_send()

        return carry

    lax.fori_loop(0, lines, sent, 0)


def solution(mesh):
    n, m = mesh.shape["context"], mesh.shape["channel"]

    def shards(inputs, out_grad, low_pass, high_pass, level_weight, mix):
        channels, length = inputs.shape
        levels = level_weight.shape[0] - 1
        width = channels // n
        rows, tokens, lines = width * m, n * length, n // 2
        count = 4 + levels + 1
        tall = -(-count // 8) * 8
        wide = -(-count // 128) * 128
        prm = jnp.concatenate([low_pass, high_pass, level_weight], 0).T
        prm = jnp.pad(prm, ((0, 0), (0, wide - count)))
        vmem = pl.BlockSpec(memory_space=pltpu.VMEM)
        f32, bf16 = jnp.float32, jnp.bfloat16
        sem = pltpu.SemaphoreType.DMA
        padded = -(-width // 128) * 128
        gi, table, gmix = pl.pallas_call(
            functools.partial(kernel, n, m, levels),
            out_shape=(
                jax.ShapeDtypeStruct((channels, length), bf16),
                jax.ShapeDtypeStruct((tall, channels), f32),
                jax.ShapeDtypeStruct((rows, channels), f32),
            ),
            in_specs=[vmem, vmem, vmem, pl.BlockSpec(memory_space=pl.ANY)],
            out_specs=(vmem,) * 3,
            scratch_shapes=[
                pltpu.VMEM((n, tall, padded), f32),
                pltpu.VMEM((n, width, length), bf16), sem((n,)), sem((n,)),
                pltpu.VMEM((n, width, length), bf16),
                pltpu.VMEM((width, wide), f32),
                pltpu.VMEM((rows, channels), bf16),
                pltpu.VMEM((n, channels, length), bf16),
                pltpu.VMEM((m, n, width, length), bf16),
                pltpu.VMEM((m, n, width, length), bf16),
                pltpu.VMEM((width, tokens), f32),
                pltpu.VMEM((levels + 2, width, tokens), f32),
                pltpu.VMEM((levels, width, tokens), f32),
                pltpu.VMEM((width, tokens), f32),
                pltpu.VMEM((width, tokens), bf16),
                pltpu.VMEM((m, width, tokens), bf16),
                pltpu.VMEM((n, width, length), bf16),
                pltpu.VMEM((padded, wide), f32),
                pltpu.VMEM((tall, padded), f32),
                sem, sem((n,)), sem((n,)), sem((n,)), sem,
                sem((lines,)), sem((lines,)), sem((lines,)), sem((lines,)), sem((n,)),
                sem((m, n)), sem((m, n)), sem((m,)), sem((m,)),
                sem((n,)), sem((n,)), sem((n,)), sem((n,)),
            ],
            compiler_params=pltpu.CompilerParams(collective_id=0, has_side_effects=True),
        )(inputs, out_grad, prm, mix)
        return gi, table[0:2], table[2:4], table[4:count], gmix

    return jax.shard_map(
        shards,
        mesh=mesh,
        in_specs=(
            P("channel", "context"),
            P("channel", "context"),
            P(None, "channel"),
            P(None, "channel"),
            P(None, "channel"),
            P(None, "channel"),
        ),
        out_specs=(
            P("channel", "context"),
            P(None, "channel"),
            P(None, "channel"),
            P(None, "channel"),
            P("context", "channel"),
        ),
        check_vma=False,
    )
```
